512 devices in a mesh: row: 16 (over y, x), col: 32 (over z, core).
Axes of the slice: x: 4, y: 4, z: 16, core: 2. Of those that a mesh axis runs over, the one named last changes fastest.
Arguments:
- inverse_sep: float32 [12288, 12288], P('row', 'col'), may hold values from -105 to 105, as said below
- sep_panels: float32 [3, 12288, 256], P(None, 'row', 'col'), may hold values from -0.0546875 to 0.0546875
- chain_panels: float32 [3, 256, 256], P(None, 'row', 'col'), may hold values from -0.375 to 0.375
- diag_inverse: float32 [3, 256, 256], P(None, 'row'), may hold values from -5 to 5, as said below
- tile_list: int32 [3, 96], replicated, may hold values from 0 to 1, as said below
Outputs:
- sep_rows: float32 [3, 256, 12288], P(None, 'row', 'col')
- chain_inverse: float32 [3, 256, 768], P(None, 'row')
The draws below stay inside these ranges and needn't reach their ends.
Inputs may be any that keep to these rules, and one draw needn't show every extreme that they name: `inverse_sep`: symmetric. `diag_inverse`: each block symmetric. `tile_list`: a tile listed for supernode k is listed for every earlier supernode.
All inputs are finite; a program needn't handle non-finite values.
Results may differ from the reference program's by a relative error of at most 0.00013.
Values sent between devices are 32-bit elements; how exact they have to be, the bound alone decides.
No kernel may reach another device: no remote copies, remote signals or barrier semaphores. Data moves between devices by JAX's collectives and lax.ppermute only.
A program may use at most 64 MiB of HBM per device.

```python
import jax
import jax.numpy as jnp
from jax import lax

NS = 12288
NB = 256
TILE = 128
NSUPER = 3
NPAIR = 3
NTILE = 96


def draw_inverse_sep(key, part):
    key_noise, key_diag = jax.random.split(jax.random.fold_in(key, 101), 2)
    noise = jnp.clip(jax.random.normal(key_noise, (NS, NS), jnp.float32), -7.0, 7.0)
    values_sym = (noise + noise.T) * 0.7071
    diag_index = jnp.arange(NS)
    return values_sym.at[diag_index, diag_index].add(jax.random.uniform(key_diag, (NS,), jnp.float32, 1.0, 4.0))


def draw_diag_inverse(key, part):
    key_noise, key_diag = jax.random.split(jax.random.fold_in(key, 202), 2)
    noise = jnp.clip(jax.random.normal(key_noise, (NSUPER, NB, NB), jnp.float32), -6.0, 6.0)
    blocks = (noise + jnp.swapaxes(noise, 1, 2)) * (0.5 / NB ** 0.5)
    diagonal = jax.random.uniform(key_diag, (NSUPER, NB), jnp.float32, 0.5, 2.0)
    return blocks + jnp.eye(NB, dtype=jnp.float32)[None] * diagonal[:, None, :]


def draw_tile_list(key, part):
    levels = jax.random.randint(jax.random.fold_in(key, 303), (NSUPER, NTILE), 0, 4)
    present = (levels > 0).astype(jnp.int32)
    return jnp.cumprod(present, axis=0).astype(jnp.int32)


def steps_of(rng, dims, pieces, least, top_value):
    loudness, own = 1.0, jax.random.fold_in(rng, 6)
    for axis_at, shards_of in pieces:
        heights = jnp.exp(jax.random.uniform(jax.random.fold_in(own, axis_at), (shards_of,), jnp.float32, least / len(pieces), top_value / len(pieces)))
        loudness = loudness * jnp.repeat(heights, dims[axis_at] // shards_of).reshape([-1 if axis == axis_at else 1 for axis in range(len(dims))])
    return loudness


def normal_values(stream_key, extent, scale, limit, pieces=(), kind=jnp.bfloat16):
    values = scale * jax.random.normal(stream_key, extent, jnp.float32)
    if pieces:
        values = values * steps_of(stream_key, extent, pieces, -0.22, 0.18)
    return jnp.clip(values, -limit, limit).astype(kind)


def setup_inputs(seed: int = 0) -> dict:
    streams_of = jax.random.split(jax.random.key(seed), 6)
    inverse_sep = draw_inverse_sep(jax.random.fold_in(streams_of[5], 71), 0)
    sep_panels = normal_values(streams_of[1], (NSUPER, NS, NB), NS ** -0.5, 0.0546875, ((1, 16), (2, 32)), jnp.float32)
    chain_panels = normal_values(streams_of[2], (NPAIR, NB, NB), NB ** -0.5, 0.375, ((1, 16), (2, 32)), jnp.float32)
    diag_inverse = draw_diag_inverse(jax.random.fold_in(streams_of[5], 71), 0)
    tile_list = draw_tile_list(jax.random.fold_in(streams_of[5], 71), 0)
    return dict(inverse_sep=inverse_sep, sep_panels=sep_panels, chain_panels=chain_panels, diag_inverse=diag_inverse, tile_list=tile_list)


def pair_index(current, earlier):
    return current * (current - 1) // 2 + earlier


def product(left, right):
    return jnp.dot(left, right, precision=lax.Precision.HIGHEST, preferred_element_type=jnp.float32)


def inner_product(left, right):
    return lax.dot_general(left, right, (((0,), (0,)), ((), ())), precision=lax.Precision.HIGHEST, preferred_element_type=jnp.float32)


def reference(inverse_sep, sep_panels, chain_panels, diag_inverse, tile_list):
    chain_state = jnp.zeros((NSUPER, NB, NSUPER * NB), jnp.float32)
    new_rows = []
    for current in range(NSUPER):
        listed = jnp.repeat(tile_list[current].astype(jnp.float32), TILE)
        panel = sep_panels[current] * listed[:, None]
        summed = inner_product(panel, inverse_sep)
        for earlier in range(current):
            summed = summed + inner_product(chain_panels[pair_index(current, earlier)], new_rows[earlier])
        rows_now = -summed
        first_term = product(rows_now, panel)
        crossing = []
        for earlier in range(current):
            crossed = product(new_rows[earlier], panel)
            for middle in range(current):
                crossed = crossed + product(chain_state[earlier, :, middle * NB:(middle + 1) * NB], chain_panels[pair_index(current, middle)])
            crossing.append(-crossed)
        second_term = jnp.zeros((NB, NB), jnp.float32)
        for earlier in range(current):
            chain_state = chain_state.at[earlier, :, current * NB:(current + 1) * NB].set(crossing[earlier])
            chain_state = chain_state.at[current, :, earlier * NB:(earlier + 1) * NB].set(crossing[earlier].T)
            second_term = second_term + product(crossing[earlier].T, chain_panels[pair_index(current, earlier)])
        chain_state = chain_state.at[current, :, current * NB:(current + 1) * NB].set(diag_inverse[current] - first_term - second_term)
        new_rows.append(rows_now)
    return jnp.stack(new_rows), chain_state
```

```python
import jax
import jax.numpy as jnp
from jax import lax
from jax.sharding import PartitionSpec as P

TILE = 128
NSUPER = 3


def contract(left, right, left_dim, right_dim):
    return lax.dot_general(
        left,
        right,
        (((left_dim,), (right_dim,)), ((), ())),
        precision=lax.Precision.HIGH,
        preferred_element_type=jnp.float32,
    )


def spread(block, axis):
    count = lax.axis_size(axis)
    copies = jnp.broadcast_to(block[None], (count,) + block.shape)
    return lax.all_to_all(copies, axis, 0, 0, tiled=True)


def per_device(inverse_sep, sep_panels, chain_panels, diag_inverse, tile_list):
    rows = lax.axis_size("row")
    cols = lax.axis_size("col")
    row = lax.axis_index("row")
    col = lax.axis_index("col")
    height, width = inverse_sep.shape
    nb_cols = sep_panels.shape[2]
    nb_rows = chain_panels.shape[1]
    nb = nb_cols * cols
    ratio = cols // rows
    core = col % ratio
    tiles = height // TILE
    npair = chain_panels.shape[0]

    listed = lax.dynamic_slice_in_dim(tile_list, row * tiles, tiles, 1).astype(jnp.float32)
    mask = jnp.broadcast_to(listed[:, :, None], (NSUPER, tiles, TILE)).reshape(NSUPER, 1, height)
    local_panel = (jnp.swapaxes(sep_panels, 1, 2) * mask).reshape(NSUPER * nb_cols, height)

    chain_local = jnp.swapaxes(chain_panels, 1, 2).reshape(1, npair * nb_cols * nb_rows)
    chain_cols = spread(chain_local, "row").reshape(rows, npair, nb_cols, nb_rows)
    chain_cols = jnp.transpose(chain_cols, (1, 2, 0, 3)).reshape(npair * nb_cols, nb)

    gathered = lax.all_gather(
        jnp.concatenate([local_panel, chain_cols], axis=1), "col", axis=0, tiled=True
    ).reshape(cols, NSUPER, nb_cols, height + nb)
    panel = [gathered[:, k, :, :height].reshape(nb, height) for k in range(NSUPER)]
    chain = [gathered[:, p, :, height:].reshape(nb, nb) for p in range(npair)]

    part = []
    for k in range(NSUPER):
        acc = contract(panel[k], inverse_sep, 1, 0)
        for j in range(k):
            acc = acc + contract(chain[k * (k - 1) // 2 + j], part[j], 1, 0)
        part.append(-acc)
    outgoing = jnp.stack([x.reshape(rows, nb_rows, width) for x in part], axis=1)
    incoming = lax.all_to_all(
        outgoing.reshape(rows, NSUPER * nb_rows, width), "row", 0, 0, tiled=True
    )
    new_rows = jnp.sum(incoming, axis=0).reshape(NSUPER, nb_rows, width)

    def route(flip):
        return [
            (r * cols + c, (c // ratio) * cols + ratio * r + ((c % ratio) ^ flip))
            for r in range(rows)
            for c in range(cols)
        ]

    lower, upper = new_rows[:, :nb_cols], new_rows[:, nb_cols:]
    same = jnp.where(core == 0, lower, upper).reshape(NSUPER * nb_cols, width)
    other = jnp.where(core == 0, upper, lower).reshape(NSUPER * nb_cols, width)
    same = lax.ppermute(same, ("row", "col"), route(0))
    other = lax.ppermute(other, ("row", "col"), route(1))
    turned = jnp.concatenate(
        [jnp.where(core == 0, same, other), jnp.where(core == 0, other, same)], axis=1
    )

    cc = chain_cols.reshape(npair, nb_cols, nb)
    place = col * nb_cols + lax.broadcasted_iota(jnp.int32, (nb_cols, nb), 0)
    unit = (lax.broadcasted_iota(jnp.int32, (nb_cols, nb), 1) == place).astype(jnp.float32)
    zero = jnp.zeros((nb_cols, nb), jnp.float32)
    solve = []
    solve.append(jnp.concatenate([unit, -cc[0], contract(cc[2], chain[0], 1, 0) - cc[1]], axis=0))
    solve.append(jnp.concatenate([zero, unit, -cc[2]], axis=0))
    solve.append(jnp.concatenate([zero, zero, unit], axis=0))
    inner = []
    for k in range(NSUPER):
        mine = lax.dynamic_slice_in_dim(solve[k], row * nb_rows, nb_rows, 1)
        acc = contract(mine, diag_inverse[k], 1, 0) - contract(turned, panel[k], 1, 1)
        for j in range(k):
            acc = acc - contract(inner[j], chain[k * (k - 1) // 2 + j], 1, 1)
        inner.append(acc)
    packed = jnp.stack(inner, axis=1).reshape(NSUPER * nb_cols, NSUPER, rows, nb_rows)
    packed = jnp.transpose(packed, (2, 0, 1, 3)).reshape(rows, 1, nb_cols * NSUPER * NSUPER * nb_rows)
    summed = jnp.sum(lax.all_to_all(packed, "row", 0, 0, tiled=True), axis=0)
    whole = spread(summed, "col").reshape(cols, NSUPER, nb_cols, NSUPER, nb_rows)
    state = jnp.transpose(whole, (3, 4, 1, 0, 2)).reshape(NSUPER, nb_rows, NSUPER * nb)
    return (new_rows, state)


def solution(mesh):
    in_specs = (
        P("row", "col"),
        P(None, "row", "col"),
        P(None, "row", "col"),
        P(None, "row", None),
        P(),
    )
    out_specs = (P(None, "row", "col"), P(None, "row", None))
    return jax.shard_map(
        per_device, mesh=mesh, in_specs=in_specs, out_specs=out_specs, check_vma=False
    )
```

```python
import jax
import jax.numpy as jnp
from jax import lax
from jax.sharding import PartitionSpec as P

TILE = 128
NSUPER = 3
NEAR = 4


def contract(left, right, left_dim, right_dim, precision=lax.Precision.HIGH):
    return lax.dot_general(
        left,
        right,
        (((left_dim,), (right_dim,)), ((), ())),
        precision=precision,
        preferred_element_type=jnp.float32,
    )


def spread(block, axis):
    count = lax.axis_size(axis)
    copies = jnp.broadcast_to(block[None], (count,) + block.shape)
    return lax.all_to_all(copies, axis, 0, 0, tiled=True)


def per_device(inverse_sep, sep_panels, chain_panels, diag_inverse, tile_list):
    rows = lax.axis_size("row")
    cols = lax.axis_size("col")
    row = lax.axis_index("row")
    col = lax.axis_index("col")
    height, width = inverse_sep.shape
    nb_cols = sep_panels.shape[2]
    nb_rows = chain_panels.shape[1]
    nb = nb_cols * cols
    cores = cols // rows
    chips = cols // cores
    far = chips // NEAR
    core = col % cores
    chip = col // cores
    tiles = height // TILE
    npair = chain_panels.shape[0]
    slab = NSUPER * nb_cols

    chain_rows = spread(chain_panels.reshape(1, npair * nb_rows * nb_cols), "col")

    listed = lax.dynamic_slice_in_dim(tile_list, row * tiles, tiles, 1).astype(jnp.float32)
    mask = jnp.broadcast_to(listed[:, :, None], (NSUPER, tiles, TILE)).reshape(NSUPER, 1, height)
    local_panel = (jnp.swapaxes(sep_panels, 1, 2) * mask).reshape(slab, height)
    far_groups = [
        [cores * (first + NEAR * i) + c for i in range(far)]
        for first in range(NEAR)
        for c in range(cores)
    ]
    own = lax.all_gather(local_panel, "col", axis=0, tiled=True, axis_index_groups=far_groups)

    chain_rows, _ = lax.optimization_barrier((chain_rows, own))
    chain_rows = chain_rows.reshape(cols, npair * nb_rows, nb_cols)
    chain_rows = jnp.transpose(chain_rows, (1, 0, 2)).reshape(npair * nb_rows, nb)
    chain_all = spread(chain_rows, "row").reshape(rows, npair, nb_rows, nb)
    chain = [chain_all[:, p].reshape(nb, nb) for p in range(npair)]

    def from_chip(block, step):
        moves = [((c + cores * step) % cols, c) for c in range(cols)]
        return lax.ppermute(block, "col", moves)

    near = [own] + [from_chip(own, step) for step in (1, 2, -1)]
    swap = [(c, c ^ 1) for c in range(cols)]
    mine = jnp.stack(near)
    theirs = lax.ppermute(mine, "col", swap)
    both = jnp.stack([jnp.where(core == 0, mine, theirs), jnp.where(core == 0, theirs, mine)])
    both = both.reshape(cores, NEAR, far, NSUPER, nb_cols, height)
    turnover = chip % NEAR
    places = []
    for place in range(NEAR):
        choice = both[:, place]
        for t in range(1, NEAR):
            choice = jnp.where(turnover == t, both[:, (place - t) % NEAR], choice)
        places.append(choice)
    ordered = jnp.stack(places)
    ordered = jnp.transpose(ordered, (3, 2, 0, 1, 4, 5)).reshape(NSUPER, nb, height)

    part = []
    for k in range(NSUPER):
        acc = contract(ordered[k], inverse_sep, 1, 0)
        for j in range(k):
            acc = acc + contract(chain[k * (k - 1) // 2 + j], part[j], 0, 0)
        part.append(-acc)
    outgoing = jnp.stack([x.reshape(rows, nb_rows, width) for x in part], axis=1)
    incoming = lax.all_to_all(
        outgoing.reshape(rows, NSUPER * nb_rows, width), "row", 0, 0, tiled=True
    )
    new_rows = jnp.sum(incoming, axis=0).reshape(NSUPER, nb_rows, width)

    solved = []
    for k in range(NSUPER):
        acc = ordered[k]
        for j in range(k):
            acc = acc - contract(chain[k * (k - 1) // 2 + j], solved[j], 0, 0)
        solved.append(acc)
    solved = jnp.concatenate(solved, axis=0).T
    place = col * nb_cols + lax.broadcasted_iota(jnp.int32, (nb_cols, nb), 0)
    unit = (lax.broadcasted_iota(jnp.int32, (nb_cols, nb), 1) == place).astype(jnp.float32)
    zero = jnp.zeros((nb_cols, nb), jnp.float32)
    cc = [contract(unit, chain[p], 1, 1, lax.Precision.HIGHEST) for p in range(npair)]
    lead = [
        jnp.concatenate([unit, -cc[0], contract(cc[2], chain[0], 1, 1) - cc[1]], axis=0),
        jnp.concatenate([zero, unit, -cc[2]], axis=0),
        jnp.concatenate([zero, zero, unit], axis=0),
    ]
    base = []
    for k in range(NSUPER):
        acc = contract(
            lax.dynamic_slice_in_dim(lead[k], row * nb_rows, nb_rows, 1), diag_inverse[k], 1, 0
        )
        for j in range(k):
            acc = acc - contract(base[j], chain[k * (k - 1) // 2 + j], 1, 0)
        base.append(acc)
    base = jnp.concatenate(base, axis=1)

    lower, upper = new_rows[:, :nb_cols], new_rows[:, nb_cols:]
    kept = jnp.where(core == 0, lower, upper).reshape(slab, width)
    sent = jnp.where(core == 0, upper, lower).reshape(slab, width)
    other = lax.ppermute(sent, "col", swap)
    wide = jnp.concatenate(
        [jnp.where(core == 0, kept, other), jnp.where(core == 0, other, kept)], axis=1
    )
    turn = [
        (r * cols + c, (c // cores) * cols + cores * r + c % cores)
        for r in range(rows)
        for c in range(cols)
    ]
    turned = lax.ppermute(wide, ("row", "col"), turn)

    inner = (base - contract(turned, solved, 1, 0)).reshape(slab, NSUPER, rows, nb_rows)
    packed = jnp.transpose(inner, (2, 0, 1, 3)).reshape(rows, 1, slab * NSUPER * nb_rows)
    summed = jnp.sum(lax.all_to_all(packed, "row", 0, 0, tiled=True), axis=0)
    whole = spread(summed, "col").reshape(cols, NSUPER, nb_cols, NSUPER, nb_rows)
    state = jnp.transpose(whole, (3, 4, 1, 0, 2)).reshape(NSUPER, nb_rows, NSUPER * nb)
    return (new_rows, state)


def solution(mesh):
    in_specs = (
        P("row", "col"),
        P(None, "row", "col"),
        P(None, "row", "col"),
        P(None, "row", None),
        P(),
    )
    out_specs = (P(None, "row", "col"), P(None, "row", None))
    return jax.shard_map(
        per_device, mesh=mesh, in_specs=in_specs, out_specs=out_specs, check_vma=False
    )
```

```python
import jax
import jax.numpy as jnp
from jax import lax
from jax.sharding import PartitionSpec as P


TILE = 128
NSUPER = 3
NEAR = 4


def contract(left, right, left_dim, right_dim, precision=lax.Precision.HIGH):
    return lax.dot_general(
        left,
        right,
        (((left_dim,), (right_dim,)), ((), ())),
        precision=precision,
        preferred_element_type=jnp.float32,
    )


def spread(block, axis):
    count = lax.axis_size(axis)
    copies = jnp.broadcast_to(block[None], (count,) + block.shape)
    return lax.all_to_all(copies, axis, 0, 0, tiled=True)


def per_device(inverse_sep, sep_panels, chain_panels, diag_inverse, tile_list):
    rows = lax.axis_size("row")
    cols = lax.axis_size("col")
    row = lax.axis_index("row")
    col = lax.axis_index("col")
    height, width = inverse_sep.shape
    nb_cols = sep_panels.shape[2]
    nb_rows = chain_panels.shape[1]
    nb = nb_cols * cols
    cores = cols // rows
    chips = cols // cores
    far = chips // NEAR
    core = col % cores
    chip = col // cores
    tiles = height // TILE
    npair = chain_panels.shape[0]
    slab = NSUPER * nb_cols

    chain_rows = spread(chain_panels.reshape(1, npair * nb_rows * nb_cols), "col")

    listed = lax.dynamic_slice_in_dim(tile_list, row * tiles, tiles, 1).astype(jnp.float32)
    mask = jnp.broadcast_to(listed[:, :, None], (NSUPER, tiles, TILE)).reshape(NSUPER, 1, height)
    local_panel = (jnp.swapaxes(sep_panels, 1, 2) * mask).reshape(slab, height)
    swap = [(c, c ^ 1) for c in range(cols)]
    turn = [
        (r * cols + c, (c // cores) * cols + cores * r + c % cores)
        for r in range(rows)
        for c in range(cols)
    ]
    turned = lax.ppermute(local_panel, ("row", "col"), turn)
    left, right = turned[:, :width], turned[:, width:]
    kept = jnp.where(core == 0, left, right)
    other = lax.ppermute(jnp.where(core == 0, right, left), "col", swap)
    pieces = jnp.stack([jnp.where(core == 0, kept, other), jnp.where(core == 0, other, kept)])
    col_panel = spread(pieces.reshape(cores * slab, width), "row")
    col_panel = col_panel.reshape(rows, cores, NSUPER, nb_cols, width)
    col_panel = [col_panel[:, :, k].reshape(nb, width) for k in range(NSUPER)]

    far_groups = [
        [cores * (first + NEAR * i) + c for i in range(far)]
        for first in range(NEAR)
        for c in range(cores)
    ]
    own = lax.all_gather(local_panel, "col", axis=0, tiled=True, axis_index_groups=far_groups)

    chain_rows, _ = lax.optimization_barrier((chain_rows, own))
    chain_rows = chain_rows.reshape(cols, npair * nb_rows, nb_cols)
    chain_rows = jnp.transpose(chain_rows, (1, 0, 2)).reshape(npair * nb_rows, nb)
    diag_cols = lax.dynamic_slice_in_dim(diag_inverse, col * nb_cols, nb_cols, 2)
    extra = NSUPER * nb_rows * nb_cols
    pad = -extra % (8 * nb)
    diag_cols = jnp.pad(diag_cols.reshape(extra), (0, pad)).reshape(-1, nb)
    chain_all = spread(jnp.concatenate([chain_rows, diag_cols], axis=0), "row")
    diag_slab = chain_all[:, npair * nb_rows :].reshape(rows, extra + pad)[:, :extra]
    diag_slab = diag_slab.reshape(rows, NSUPER, nb_rows, nb_cols)
    diag_slab = [diag_slab[:, k].reshape(nb, nb_cols) for k in range(NSUPER)]
    chain_all = chain_all[:, : npair * nb_rows].reshape(rows, npair, nb_rows, nb)
    chain = [chain_all[:, p].reshape(nb, nb) for p in range(npair)]

    def from_chip(block, step):
        moves = [((c + cores * step) % cols, c) for c in range(cols)]
        return lax.ppermute(block, "col", moves)

    near = [own] + [from_chip(own, step) for step in (1, 2, -1)]
    mine = jnp.stack(near)
    theirs = lax.ppermute(mine, "col", swap)
    both = jnp.stack([jnp.where(core == 0, mine, theirs), jnp.where(core == 0, theirs, mine)])
    both = both.reshape(cores, NEAR, far, NSUPER, nb_cols, height)
    turnover = chip % NEAR
    places = []
    for place in range(NEAR):
        choice = both[:, place]
        for t in range(1, NEAR):
            choice = jnp.where(turnover == t, both[:, (place - t) % NEAR], choice)
        places.append(choice)
    ordered = jnp.stack(places)
    ordered = jnp.transpose(ordered, (3, 2, 0, 1, 4, 5)).reshape(NSUPER, nb, height)

    part = []
    for k in range(NSUPER):
        acc = contract(ordered[k], inverse_sep, 1, 0)
        for j in range(k):
            acc = acc + contract(chain[k * (k - 1) // 2 + j], part[j], 0, 0)
        part.append(-acc)
    outgoing = jnp.stack([x.reshape(rows, nb_rows, width) for x in part], axis=1)
    incoming = lax.all_to_all(
        outgoing.reshape(rows, NSUPER * nb_rows, width), "row", 0, 0, tiled=True
    )
    new_rows = jnp.sum(incoming, axis=0).reshape(NSUPER, nb_rows, width)

    exact = lax.Precision.HIGHEST
    solved = []
    for k in range(NSUPER):
        acc = col_panel[k]
        for j in range(k):
            acc = acc - contract(chain[k * (k - 1) // 2 + j], solved[j], 0, 0)
        solved.append(acc)
    solved = jnp.concatenate(solved, axis=0)
    place = row * nb_rows + lax.broadcasted_iota(jnp.int32, (nb_rows, nb), 0)
    unit = (lax.broadcasted_iota(jnp.int32, (nb_rows, nb), 1) == place).astype(jnp.float32)
    zero = jnp.zeros((nb_rows, nb), jnp.float32)
    cc = [contract(unit, chain[p], 1, 1, exact) for p in range(npair)]
    lead = [
        jnp.concatenate([unit, -cc[0], contract(cc[2], chain[0], 1, 1, exact) - cc[1]], axis=0),
        jnp.concatenate([zero, unit, -cc[2]], axis=0),
        jnp.concatenate([zero, zero, unit], axis=0),
    ]
    base = []
    for k in range(NSUPER):
        part_lead = lax.dynamic_slice_in_dim(lead[k], col * nb_cols, nb_cols, 1)
        acc = contract(part_lead, diag_slab[k], 1, 1, exact)
        for j in range(k):
            acc = acc - contract(base[j], chain[k * (k - 1) // 2 + j], 1, 0, exact)
        base.append(acc)
    base = jnp.concatenate(base, axis=1)

    inner = base - contract(new_rows.reshape(NSUPER * nb_rows, width), solved, 1, 1)
    share = NSUPER * nb_rows * NSUPER * nb // cols
    summed = jnp.sum(lax.all_to_all(inner.reshape(cols, 1, share), "col", 0, 0, tiled=True), axis=0)
    state = spread(summed, "col").reshape(NSUPER, nb_rows, NSUPER * nb)
    return (new_rows, state)


def solution(mesh):
    in_specs = (
        P("row", "col"),
        P(None, "row", "col"),
        P(None, "row", "col"),
        P(None, "row", None),
        P(),
    )
    out_specs = (P(None, "row", "col"), P(None, "row", None))

    return jax.shard_map(
        per_device, mesh=mesh, in_specs=in_specs, out_specs=out_specs, check_vma=False
    )
```

```python
import jax
import jax.numpy as jnp
from jax import lax
from jax.sharding import PartitionSpec as P


TILE = 128
NSUPER = 3
NEAR = 4
LANES = 128


def contract(left, right, left_dim, right_dim, precision=lax.Precision.HIGH):
    return lax.dot_general(
        left,
        right,
        (((left_dim,), (right_dim,)), ((), ())),
        precision=precision,
        preferred_element_type=jnp.float32,
    )


def exchange(blocks, axis, groups=None):
    return lax.all_to_all(blocks, axis, 0, 0, tiled=True, axis_index_groups=groups)


def spread(block, axis, groups=None):
    count = len(groups[0]) if groups else lax.axis_size(axis)
    return exchange(jnp.broadcast_to(block[None], (count,) + block.shape), axis, groups)


def per_device(inverse_sep, sep_panels, chain_panels, diag_inverse, tile_list):
    rows = lax.axis_size("row")
    cols = lax.axis_size("col")
    row = lax.axis_index("row")
    col = lax.axis_index("col")
    height, width = inverse_sep.shape
    nb_cols = sep_panels.shape[2]
    nb_rows = chain_panels.shape[1]
    nb = nb_cols * cols
    cores = cols // rows
    chips = cols // cores
    far = chips // NEAR
    core = col % cores
    chip = col // cores
    tiles = height // TILE
    npair = chain_panels.shape[0]
    slab = NSUPER * nb_cols
    own_rows = NSUPER * nb_rows
    far_groups = [
        [cores * (first + NEAR * i) + c for i in range(far)]
        for first in range(NEAR)
        for c in range(cores)
    ]
    near_groups = [
        [cores * (NEAR * i + j) + c for j in range(NEAR) for c in range(cores)] for i in range(far)
    ]
    swap = [(c, c ^ 1) for c in range(cols)]
    turn = [
        (r * cols + c, (c // cores) * cols + cores * r + c % cores)
        for r in range(rows)
        for c in range(cols)
    ]

    listed = lax.dynamic_slice_in_dim(tile_list, row * tiles, tiles, 1).astype(jnp.float32)
    mask = jnp.broadcast_to(listed[:, :, None], (NSUPER, tiles, TILE)).reshape(NSUPER, 1, height)
    local_panel = (jnp.swapaxes(sep_panels, 1, 2) * mask).reshape(slab, height)
    turned = lax.ppermute(local_panel, ("row", "col"), turn)

    chain_size = npair * nb_rows * nb_cols
    chain_lines = chain_size // LANES
    chain_flat = chain_panels.reshape(chain_lines, LANES)
    chain_flat = jnp.pad(chain_flat, ((0, slab - chain_lines), (0, 0)))
    own = lax.all_gather(
        jnp.concatenate([local_panel, chain_flat], axis=1),
        "col",
        axis=0,
        tiled=True,
        axis_index_groups=far_groups,
    )
    chain_own = own[:, height:].reshape(far, slab, LANES)[:, :chain_lines]
    own = own[:, :height]

    chain_rows = spread(chain_own.reshape(1, far * chain_size), "col", near_groups)
    chain_rows = chain_rows.reshape(NEAR, cores, far, npair * nb_rows, nb_cols)
    chain_rows = jnp.transpose(chain_rows, (3, 2, 0, 1, 4)).reshape(npair * nb_rows, nb)
    diag_cols = lax.dynamic_slice_in_dim(diag_inverse, col * nb_cols, nb_cols, 2)
    diag_cols = jnp.concatenate([diag_cols[k] for k in range(NSUPER)], axis=1)
    diag_cols = jnp.pad(diag_cols, ((0, 0), (0, LANES - slab)))

    left, right = turned[:, :width], turned[:, width:]
    kept = jnp.where(core == 0, left, right)
    other = lax.ppermute(jnp.where(core == 0, right, left), "col", swap)
    pieces = [jnp.where(core == 0, kept, other), jnp.where(core == 0, other, kept)]
    pieces = jnp.concatenate(pieces, axis=0)

    def lines(block):
        tiles = range(0, block.shape[1], LANES)
        return jnp.concatenate([block[:, t : t + LANES] for t in tiles], axis=0)

    sides = [lines(chain_rows), diag_cols, lines(pieces)]
    sides_all = spread(jnp.concatenate(sides, axis=0), "row")
    cut = [sides[0].shape[0], sides[0].shape[0] + sides[1].shape[0]]
    chain_all = sides_all[:, : cut[0]].reshape(rows, nb // LANES, npair, nb_rows, LANES)
    chain = [
        jnp.concatenate(
            [chain_all[:, t, p].reshape(nb, LANES) for t in range(nb // LANES)], axis=1
        )
        for p in range(npair)
    ]
    late_sides = sides_all[:, cut[0] :]

    def from_chip(block, step):
        moves = [((c + cores * step) % cols, c) for c in range(cols)]
        return lax.ppermute(block, "col", moves)

    near = [own] + [from_chip(own, step) for step in (1, 2, -1)]
    mine = jnp.stack(near)
    theirs = lax.ppermute(mine, "col", swap)
    both = jnp.stack([jnp.where(core == 0, mine, theirs), jnp.where(core == 0, theirs, mine)])
    both = both.reshape(cores, NEAR, far, NSUPER, nb_cols, height)
    turnover = chip % NEAR
    places = []
    for place in range(NEAR):
        choice = both[:, place]
        for t in range(1, NEAR):
            choice = jnp.where(turnover == t, both[:, (place - t) % NEAR], choice)
        places.append(choice)
    ordered = jnp.stack(places)
    ordered = jnp.transpose(ordered, (3, 2, 0, 1, 4, 5)).reshape(NSUPER, nb, height)

    part = []
    for k in range(NSUPER):
        acc = contract(ordered[k], inverse_sep, 1, 0)
        for j in range(k):
            acc = acc + contract(chain[k * (k - 1) // 2 + j], part[j], 0, 0)
        part.append(-acc)
    outgoing = jnp.stack([x.reshape(rows, nb_rows, width) for x in part], axis=1)
    incoming = exchange(outgoing.reshape(rows, own_rows, width), "row")
    new_rows = jnp.sum(incoming, axis=0)

    col_panel = late_sides[:, nb_rows:].reshape(rows, width // LANES, cores, NSUPER, nb_cols, LANES)
    col_panel = [
        jnp.concatenate(
            [col_panel[:, t, :, k].reshape(nb, LANES) for t in range(width // LANES)], axis=1
        )
        for k in range(NSUPER)
    ]
    solved = []
    for k in range(NSUPER):
        acc = col_panel[k]
        for j in range(k):
            acc = acc - contract(chain[k * (k - 1) // 2 + j], solved[j], 0, 0)
        solved.append(acc)
    solved = jnp.concatenate(solved, axis=0)
    exact = lax.Precision.HIGHEST
    place = row * nb_rows + lax.broadcasted_iota(jnp.int32, (nb_rows, nb), 0)
    unit = (lax.broadcasted_iota(jnp.int32, (nb_rows, nb), 1) == place).astype(jnp.float32)
    zero = jnp.zeros((nb_rows, nb), jnp.float32)
    cc = [contract(unit, chain[p], 1, 1, exact) for p in range(npair)]
    lead = [
        jnp.concatenate([unit, -cc[0], contract(cc[2], chain[0], 1, 1, exact) - cc[1]], axis=0),
        jnp.concatenate([zero, unit, -cc[2]], axis=0),
        jnp.concatenate([zero, zero, unit], axis=0),
    ]
    diag_all = late_sides[:, :nb_rows].reshape(nb, LANES)
    source = lax.broadcasted_iota(jnp.int32, (nb, LANES), 0) - col * nb_cols
    target = lax.broadcasted_iota(jnp.int32, (nb, LANES), 1)
    inside = (source >= 0) & (source < nb_cols)
    base = []
    for k in range(NSUPER):
        pick = (inside & (target == source + k * nb_cols)).astype(jnp.float32)
        acc = contract(contract(lead[k], pick, 1, 0, exact), diag_all, 1, 1, exact)
        for j in range(k):
            acc = acc - contract(base[j], chain[k * (k - 1) // 2 + j], 1, 0, exact)
        base.append(acc)
    base = jnp.concatenate(base, axis=1)

    inner = base - contract(new_rows, solved, 1, 1)
    share = own_rows * NSUPER * nb // (NEAR * cores)
    near_sum = jnp.sum(exchange(inner.reshape(NEAR * cores, 1, share), "col", near_groups), axis=0)
    far_sum = jnp.sum(spread(near_sum, "col", far_groups), axis=0)
    state = spread(far_sum, "col", near_groups)
    return (
        new_rows.reshape(NSUPER, nb_rows, width),
        state.reshape(NSUPER, nb_rows, NSUPER * nb),
    )


def solution(mesh):
    in_specs = (
        P("row", "col"),
        P(None, "row", "col"),
        P(None, "row", "col"),
        P(None, "row", None),
        P(),
    )
    out_specs = (P(None, "row", "col"), P(None, "row", None))

    return jax.shard_map(
        per_device, mesh=mesh, in_specs=in_specs, out_specs=out_specs, check_vma=False
    )
```

```python
import jax
import jax.numpy as jnp
from jax import lax
from jax.sharding import PartitionSpec as P


TILE = 128
NSUPER = 3
NEAR = 4
LANES = 128


def contract(left, right, left_dim, right_dim, precision=lax.Precision.HIGH):
    return lax.dot_general(
        left,
        right,
        (((left_dim,), (right_dim,)), ((), ())),
        precision=precision,
        preferred_element_type=jnp.float32,
    )


def exchange(blocks, axis, groups=None):
    return lax.all_to_all(blocks, axis, 0, 0, tiled=True, axis_index_groups=groups)


def spread(block, axis, groups=None):
    count = len(groups[0]) if groups else lax.axis_size(axis)
    return exchange(jnp.broadcast_to(block[None], (count,) + block.shape), axis, groups)


def per_device(inverse_sep, sep_panels, chain_panels, diag_inverse, tile_list):
    rows = lax.axis_size("row")
    cols = lax.axis_size("col")
    row = lax.axis_index("row")
    col = lax.axis_index("col")
    height, width = inverse_sep.shape
    nb_cols = sep_panels.shape[2]
    nb_rows = chain_panels.shape[1]
    nb = nb_cols * cols
    cores = cols // rows
    chips = cols // cores
    far = chips // NEAR
    core = col % cores
    chip = col // cores
    tiles = height // TILE
    npair = chain_panels.shape[0]
    slab = NSUPER * nb_cols
    own_rows = NSUPER * nb_rows
    far_groups = [
        [cores * (first + NEAR * i) + c for i in range(far)]
        for first in range(NEAR)
        for c in range(cores)
    ]
    near_groups = [
        [cores * (NEAR * i + j) + c for j in range(NEAR) for c in range(cores)] for i in range(far)
    ]
    swap = [(c, c ^ 1) for c in range(cols)]
    turn = [
        (r * cols + c, (c // cores) * cols + cores * r + c % cores)
        for r in range(rows)
        for c in range(cols)
    ]

    listed = lax.dynamic_slice_in_dim(tile_list, row * tiles, tiles, 1).astype(jnp.float32)
    mask = jnp.broadcast_to(listed[:, :, None], (NSUPER, tiles, TILE)).reshape(NSUPER, 1, height)
    local_panel = (jnp.swapaxes(sep_panels, 1, 2) * mask).reshape(slab, height)
    turned = lax.ppermute(local_panel, ("row", "col"), turn)

    chain_size = npair * nb_rows * nb_cols
    chain_lines = chain_size // LANES
    chain_flat = chain_panels.reshape(chain_lines, LANES)
    chain_flat = jnp.pad(chain_flat, ((0, slab - chain_lines), (0, 0)))
    own = lax.all_gather(
        jnp.concatenate([local_panel, chain_flat], axis=1),
        "col",
        axis=0,
        tiled=True,
        axis_index_groups=far_groups,
    )
    chain_own = own[:, height:].reshape(far, slab, LANES)[:, :chain_lines]
    own = own[:, :height]

    chain_rows = spread(chain_own.reshape(1, far * chain_size), "col", near_groups)
    chain_rows = chain_rows.reshape(NEAR, cores, far, npair * nb_rows, nb_cols)
    chain_rows = jnp.transpose(chain_rows, (3, 2, 0, 1, 4)).reshape(npair * nb_rows, nb)
    diag_cols = lax.dynamic_slice_in_dim(diag_inverse, col * nb_cols, nb_cols, 2)
    diag_cols = jnp.concatenate([diag_cols[k] for k in range(NSUPER)], axis=1)
    diag_cols = jnp.pad(diag_cols, ((0, 0), (0, LANES - slab)))

    left, right = turned[:, :width], turned[:, width:]
    kept = jnp.where(core == 0, left, right)
    other = lax.ppermute(jnp.where(core == 0, right, left), "col", swap)
    pieces = [jnp.where(core == 0, kept, other), jnp.where(core == 0, other, kept)]
    pieces = jnp.concatenate(pieces, axis=0)

    def lines(block):
        tiles = range(0, block.shape[1], LANES)
        return jnp.concatenate([block[:, t : t + LANES] for t in tiles], axis=0)

    chain_lines = lines(chain_rows)
    chain_all = spread(jnp.concatenate([chain_lines, diag_cols], axis=0), "row")
    col_panel = spread(pieces, "row").reshape(rows, cores, NSUPER, nb_cols, width)
    diag_all = chain_all[:, chain_lines.shape[0] :].reshape(nb, LANES)
    chain_all = chain_all[:, : chain_lines.shape[0]]
    chain_all = chain_all.reshape(rows, nb // LANES, npair, nb_rows, LANES)
    chain = [
        jnp.concatenate(
            [chain_all[:, t, p].reshape(nb, LANES) for t in range(nb // LANES)], axis=1
        )
        for p in range(npair)
    ]

    def from_chip(block, step):
        moves = [((c + cores * step) % cols, c) for c in range(cols)]
        return lax.ppermute(block, "col", moves)

    near = [own] + [from_chip(own, step) for step in (1, 2, -1)]
    mine = jnp.stack(near)
    theirs = lax.ppermute(mine, "col", swap)
    both = jnp.stack([jnp.where(core == 0, mine, theirs), jnp.where(core == 0, theirs, mine)])
    both = both.reshape(cores, NEAR, far, NSUPER, nb_cols, height)
    turnover = chip % NEAR
    places = []
    for place in range(NEAR):
        choice = both[:, place]
        for t in range(1, NEAR):
            choice = jnp.where(turnover == t, both[:, (place - t) % NEAR], choice)
        places.append(choice)
    ordered = jnp.stack(places)
    ordered = jnp.transpose(ordered, (3, 2, 0, 1, 4, 5)).reshape(NSUPER, nb, height)

    part = []
    for k in range(NSUPER):
        acc = contract(ordered[k], inverse_sep, 1, 0)
        for j in range(k):
            acc = acc + contract(chain[k * (k - 1) // 2 + j], part[j], 0, 0)
        part.append(-acc)
    outgoing = jnp.stack([x.reshape(rows, nb_rows, width) for x in part], axis=1)
    incoming = exchange(outgoing.reshape(rows, own_rows, width), "row")
    new_rows = jnp.sum(incoming, axis=0)

    col_panel = [col_panel[:, :, k].reshape(nb, width) for k in range(NSUPER)]
    solved = []
    for k in range(NSUPER):
        acc = col_panel[k]
        for j in range(k):
            acc = acc - contract(chain[k * (k - 1) // 2 + j], solved[j], 0, 0)
        solved.append(acc)
    solved = jnp.concatenate(solved, axis=0)
    exact = lax.Precision.HIGHEST
    place = row * nb_rows + lax.broadcasted_iota(jnp.int32, (nb_rows, nb), 0)
    unit = (lax.broadcasted_iota(jnp.int32, (nb_rows, nb), 1) == place).astype(jnp.float32)
    zero = jnp.zeros((nb_rows, nb), jnp.float32)
    cc = [contract(unit, chain[p], 1, 1, exact) for p in range(npair)]
    lead = [
        jnp.concatenate([unit, -cc[0], contract(cc[2], chain[0], 1, 1, exact) - cc[1]], axis=0),
        jnp.concatenate([zero, unit, -cc[2]], axis=0),
        jnp.concatenate([zero, zero, unit], axis=0),
    ]
    source = lax.broadcasted_iota(jnp.int32, (nb, LANES), 0) - col * nb_cols
    target = lax.broadcasted_iota(jnp.int32, (nb, LANES), 1)
    inside = (source >= 0) & (source < nb_cols)
    base = []
    for k in range(NSUPER):
        pick = (inside & (target == source + k * nb_cols)).astype(jnp.float32)
        acc = contract(contract(lead[k], pick, 1, 0, exact), diag_all, 1, 1, exact)
        for j in range(k):
            acc = acc - contract(base[j], chain[k * (k - 1) // 2 + j], 1, 0, exact)
        base.append(acc)
    base = jnp.concatenate(base, axis=1)

    inner = base - contract(new_rows, solved, 1, 1)
    share = own_rows * NSUPER * nb // (NEAR * cores)
    near_sum = jnp.sum(exchange(inner.reshape(NEAR * cores, 1, share), "col", near_groups), axis=0)
    far_sum = jnp.sum(spread(near_sum, "col", far_groups), axis=0)
    state = spread(far_sum, "col", near_groups)
    return (
        new_rows.reshape(NSUPER, nb_rows, width),
        state.reshape(NSUPER, nb_rows, NSUPER * nb),
    )


def solution(mesh):
    in_specs = (
        P("row", "col"),
        P(None, "row", "col"),
        P(None, "row", "col"),
        P(None, "row", None),
        P(),
    )
    out_specs = (P(None, "row", "col"), P(None, "row", None))

    return jax.shard_map(
        per_device, mesh=mesh, in_specs=in_specs, out_specs=out_specs, check_vma=False
    )
```

```python
import jax
import jax.numpy as jnp
from jax import lax
from jax.sharding import PartitionSpec as P


TILE = 128
NSUPER = 3
NEAR = 4


def contract(left, right, left_dim, right_dim, precision=lax.Precision.HIGH):
    return lax.dot_general(
        left,
        right,
        (((left_dim,), (right_dim,)), ((), ())),
        precision=precision,
        preferred_element_type=jnp.float32,
    )


def exchange(blocks, axis, groups=None):
    return lax.all_to_all(blocks, axis, 0, 0, tiled=True, axis_index_groups=groups)


def spread(block, axis, groups=None):
    count = len(groups[0]) if groups else lax.axis_size(axis)
    return exchange(jnp.broadcast_to(block[None], (count,) + block.shape), axis, groups)


def per_device(inverse_sep, sep_panels, chain_panels, diag_inverse, tile_list):
    rows = lax.axis_size("row")
    cols = lax.axis_size("col")
    row = lax.axis_index("row")
    col = lax.axis_index("col")
    height, width = inverse_sep.shape
    nb_cols = sep_panels.shape[2]
    nb_rows = chain_panels.shape[1]
    nb = nb_cols * cols
    cores = cols // rows
    chips = cols // cores
    far = chips // NEAR
    core = col % cores
    chip = col // cores
    tiles = height // TILE
    npair = chain_panels.shape[0]
    slab = NSUPER * nb_cols
    own_rows = NSUPER * nb_rows
    far_groups = [
        [cores * (first + NEAR * i) + c for i in range(far)]
        for first in range(NEAR)
        for c in range(cores)
    ]
    near_groups = [
        [cores * (NEAR * i + j) + c for j in range(NEAR) for c in range(cores)] for i in range(far)
    ]
    swap = [(c, c ^ 1) for c in range(cols)]
    turn = [
        (r * cols + c, (c // cores) * cols + cores * r + c % cores)
        for r in range(rows)
        for c in range(cols)
    ]

    listed = lax.dynamic_slice_in_dim(tile_list, row * tiles, tiles, 1).astype(jnp.float32)
    mask = jnp.broadcast_to(listed[:, :, None], (NSUPER, tiles, TILE)).reshape(NSUPER, 1, height)
    local_panel = (jnp.swapaxes(sep_panels, 1, 2) * mask).reshape(slab, height)
    diag_cols = lax.dynamic_slice_in_dim(diag_inverse, col * nb_cols, nb_cols, 2)
    small = jnp.concatenate([chain_panels, diag_cols], axis=0)
    small_rows = (npair + NSUPER) * nb_cols
    small = jnp.swapaxes(small, 1, 2).reshape(1, small_rows * nb_rows)
    small = spread(small, "row").reshape(rows, small_rows, nb_rows)
    small = jnp.transpose(small, (1, 0, 2)).reshape(small_rows, nb)
    chain_cols, diag_cols = small[: npair * nb_cols], small[npair * nb_cols :]
    turned = lax.ppermute(local_panel, ("row", "col"), turn)

    own = lax.all_gather(
        jnp.concatenate([local_panel, chain_cols], axis=1),
        "col",
        axis=0,
        tiled=True,
        axis_index_groups=far_groups,
    )

    left, right = turned[:, :width], turned[:, width:]
    kept = jnp.where(core == 0, left, right)
    other = lax.ppermute(jnp.where(core == 0, right, left), "col", swap)
    pieces = [jnp.where(core == 0, kept, other), jnp.where(core == 0, other, kept)]
    col_panel = spread(jnp.concatenate(pieces, axis=0), "row")
    col_panel = col_panel.reshape(rows, cores, NSUPER, nb_cols, width)

    def from_chip(block, step):
        moves = [((c + cores * step) % cols, c) for c in range(cols)]
        return lax.ppermute(block, "col", moves)

    near = [own] + [from_chip(own, step) for step in (1, 2, -1)]
    mine = jnp.stack(near)
    theirs = lax.ppermute(mine, "col", swap)
    both = jnp.stack([jnp.where(core == 0, mine, theirs), jnp.where(core == 0, theirs, mine)])
    both = both.reshape(cores, NEAR, far, NSUPER, nb_cols, height + nb)
    turnover = chip % NEAR
    places = []
    for place in range(NEAR):
        choice = both[:, place]
        for t in range(1, NEAR):
            choice = jnp.where(turnover == t, both[:, (place - t) % NEAR], choice)
        places.append(choice)
    ordered = jnp.stack(places)
    ordered = jnp.transpose(ordered, (3, 2, 0, 1, 4, 5)).reshape(NSUPER, nb, height + nb)
    panel = [ordered[k, :, :height] for k in range(NSUPER)]
    chain = [ordered[p, :, height:] for p in range(npair)]

    part = []
    for k in range(NSUPER):
        acc = contract(panel[k], inverse_sep, 1, 0)
        for j in range(k):
            acc = acc + contract(chain[k * (k - 1) // 2 + j], part[j], 1, 0)
        part.append(-acc)
    outgoing = jnp.stack([x.reshape(rows, nb_rows, width) for x in part], axis=1)
    incoming = exchange(outgoing.reshape(rows, own_rows, width), "row")
    new_rows = jnp.sum(incoming, axis=0)

    col_panel = [col_panel[:, :, k].reshape(nb, width) for k in range(NSUPER)]
    solved = []
    for k in range(NSUPER):
        acc = col_panel[k]
        for j in range(k):
            acc = acc - contract(chain[k * (k - 1) // 2 + j], solved[j], 1, 0)
        solved.append(acc)
    solved = jnp.concatenate(solved, axis=0)
    exact = lax.Precision.HIGHEST
    place = row * nb_rows + lax.broadcasted_iota(jnp.int32, (nb_rows, nb), 0)
    unit = (lax.broadcasted_iota(jnp.int32, (nb_rows, nb), 1) == place).astype(jnp.float32)
    zero = jnp.zeros((nb_rows, nb), jnp.float32)
    cc = [lax.dynamic_slice_in_dim(chain[p], row * nb_rows, nb_rows, 0) for p in range(npair)]
    lead = [
        jnp.concatenate([unit, -cc[0], contract(cc[2], chain[0], 1, 0, exact) - cc[1]], axis=0),
        jnp.concatenate([zero, unit, -cc[2]], axis=0),
        jnp.concatenate([zero, zero, unit], axis=0),
    ]
    base = []
    for k in range(NSUPER):
        part_lead = lax.dynamic_slice_in_dim(lead[k], col * nb_cols, nb_cols, 1)
        acc = contract(part_lead, diag_cols[k * nb_cols : (k + 1) * nb_cols], 1, 0, exact)
        for j in range(k):
            acc = acc - contract(base[j], chain[k * (k - 1) // 2 + j], 1, 1, exact)
        base.append(acc)
    base = jnp.concatenate(base, axis=1)

    inner = base - contract(new_rows, solved, 1, 1)
    share = own_rows * NSUPER * nb // (NEAR * cores)
    near_sum = jnp.sum(exchange(inner.reshape(NEAR * cores, 1, share), "col", near_groups), axis=0)
    far_sum = jnp.sum(spread(near_sum, "col", far_groups), axis=0)
    state = spread(far_sum, "col", near_groups)
    return (
        new_rows.reshape(NSUPER, nb_rows, width),
        state.reshape(NSUPER, nb_rows, NSUPER * nb),
    )


def solution(mesh):
    in_specs = (
        P("row", "col"),
        P(None, "row", "col"),
        P(None, "row", "col"),
        P(None, "row", None),
        P(),
    )
    out_specs = (P(None, "row", "col"), P(None, "row", None))

    return jax.shard_map(
        per_device, mesh=mesh, in_specs=in_specs, out_specs=out_specs, check_vma=False
    )
```

```python
import jax
import jax.numpy as jnp
from jax import lax
from jax.sharding import PartitionSpec as P


TILE = 128
NSUPER = 3
NEAR = 4


def contract(left, right, left_dim, right_dim, precision=lax.Precision.HIGH):
    return lax.dot_general(
        left,
        right,
        (((left_dim,), (right_dim,)), ((), ())),
        precision=precision,
        preferred_element_type=jnp.float32,
    )


def exchange(blocks, axis, groups=None):
    return lax.all_to_all(blocks, axis, 0, 0, tiled=True, axis_index_groups=groups)


def spread(block, axis, groups=None):
    count = len(groups[0]) if groups else lax.axis_size(axis)
    return exchange(jnp.broadcast_to(block[None], (count,) + block.shape), axis, groups)


def per_device(inverse_sep, sep_panels, chain_panels, diag_inverse, tile_list):
    rows = lax.axis_size("row")
    cols = lax.axis_size("col")
    row = lax.axis_index("row")
    col = lax.axis_index("col")
    height, width = inverse_sep.shape
    nb_cols = sep_panels.shape[2]
    nb_rows = chain_panels.shape[1]
    nb = nb_cols * cols
    cores = cols // rows
    chips = cols // cores
    far = chips // NEAR
    core = col % cores
    chip = col // cores
    tiles = height // TILE
    npair = chain_panels.shape[0]
    slab = NSUPER * nb_cols
    own_rows = NSUPER * nb_rows
    far_groups = [
        [cores * (first + NEAR * i) + c for i in range(far)]
        for first in range(NEAR)
        for c in range(cores)
    ]
    near_groups = [
        [cores * (NEAR * i + j) + c for j in range(NEAR) for c in range(cores)] for i in range(far)
    ]
    swap = [(c, c ^ 1) for c in range(cols)]
    turn = [
        (r * cols + c, (c // cores) * cols + cores * r + c % cores)
        for r in range(rows)
        for c in range(cols)
    ]

    listed = lax.dynamic_slice_in_dim(tile_list, row * tiles, tiles, 1).astype(jnp.float32)
    mask = jnp.broadcast_to(listed[:, :, None], (NSUPER, tiles, TILE)).reshape(NSUPER, 1, height)
    local_panel = (jnp.swapaxes(sep_panels, 1, 2) * mask).reshape(slab, height)
    diag_cols = lax.dynamic_slice_in_dim(diag_inverse, col * nb_cols, nb_cols, 2)
    small = jnp.concatenate([chain_panels, diag_cols], axis=0)
    small_rows = (npair + NSUPER) * nb_cols
    small = jnp.swapaxes(small, 1, 2).reshape(1, small_rows * nb_rows)
    small = spread(small, "row").reshape(rows, small_rows, nb_rows)
    small = jnp.transpose(small, (1, 0, 2)).reshape(small_rows, nb)
    small = lax.optimization_barrier(small)
    chain_cols, diag_cols = small[: npair * nb_cols], small[npair * nb_cols :]
    turned = lax.ppermute(local_panel, ("row", "col"), turn)

    own = lax.all_gather(
        jnp.concatenate([local_panel, chain_cols], axis=1),
        "col",
        axis=0,
        tiled=True,
        axis_index_groups=far_groups,
    )

    left, right = turned[:, :width], turned[:, width:]
    kept = jnp.where(core == 0, left, right)
    other = lax.ppermute(jnp.where(core == 0, right, left), "col", swap)
    pieces = [jnp.where(core == 0, kept, other), jnp.where(core == 0, other, kept)]
    col_panel = spread(jnp.concatenate(pieces, axis=0), "row")
    col_panel = col_panel.reshape(rows, cores, NSUPER, nb_cols, width)

    def from_chip(block, step):
        moves = [((c + cores * step) % cols, c) for c in range(cols)]
        return lax.ppermute(block, "col", moves)

    near = [own] + [from_chip(own, step) for step in (1, 2, -1)]
    mine = jnp.stack(near)
    theirs = lax.ppermute(mine, "col", swap)
    both = jnp.stack([jnp.where(core == 0, mine, theirs), jnp.where(core == 0, theirs, mine)])
    both = both.reshape(cores, NEAR, far, NSUPER, nb_cols, height + nb)
    turnover = chip % NEAR
    places = []
    for place in range(NEAR):
        choice = both[:, place]
        for t in range(1, NEAR):
            choice = jnp.where(turnover == t, both[:, (place - t) % NEAR], choice)
        places.append(choice)
    ordered = jnp.stack(places)
    ordered = jnp.transpose(ordered, (3, 2, 0, 1, 4, 5)).reshape(NSUPER, nb, height + nb)
    panel = [ordered[k, :, :height] for k in range(NSUPER)]
    chain = [ordered[p, :, height:] for p in range(npair)]

    part = []
    for k in range(NSUPER):
        acc = contract(panel[k], inverse_sep, 1, 0)
        for j in range(k):
            acc = acc + contract(chain[k * (k - 1) // 2 + j], part[j], 1, 0)
        part.append(-acc)
    outgoing = jnp.stack([x.reshape(rows, nb_rows, width) for x in part], axis=1)
    incoming = exchange(outgoing.reshape(rows, own_rows, width), "row")
    new_rows = jnp.sum(incoming, axis=0)

    exact = lax.Precision.HIGHEST
    col_panel = jnp.concatenate(
        [col_panel[:, :, k].reshape(nb, width) for k in range(NSUPER)], axis=0
    )
    place = row * nb_rows + lax.broadcasted_iota(jnp.int32, (nb_rows, nb), 0)
    unit = (lax.broadcasted_iota(jnp.int32, (nb_rows, nb), 1) == place).astype(jnp.float32)
    zero = jnp.zeros((nb_rows, nb), jnp.float32)
    cc = [lax.dynamic_slice_in_dim(chain[p], row * nb_rows, nb_rows, 0) for p in range(npair)]
    lead = [
        jnp.concatenate([unit, -cc[0], contract(cc[2], chain[0], 1, 0, exact) - cc[1]], axis=0),
        jnp.concatenate([zero, unit, -cc[2]], axis=0),
        jnp.concatenate([zero, zero, unit], axis=0),
    ]
    base = []
    for k in range(NSUPER):
        part_lead = lax.dynamic_slice_in_dim(lead[k], col * nb_cols, nb_cols, 1)
        diag_part = diag_cols[k * nb_cols : (k + 1) * nb_cols]
        base.append(contract(part_lead, diag_part, 1, 0, exact))
    base = jnp.concatenate(base, axis=1)

    inner = base - contract(new_rows, col_panel, 1, 1)
    members = NEAR * cores
    share = own_rows * NSUPER * nb // members
    near_sum = jnp.sum(exchange(inner.reshape(members, 1, share), "col", near_groups), axis=0)
    far_sum = jnp.sum(spread(near_sum, "col", far_groups), axis=0)
    far_sum = far_sum.reshape(own_rows // members, NSUPER, nb)
    final = []
    for k in range(NSUPER):
        acc = far_sum[:, k]
        for j in range(k):
            acc = acc - contract(final[j], chain[k * (k - 1) // 2 + j], 1, 1)
        final.append(acc)
    state = spread(jnp.stack(final, axis=1).reshape(1, share), "col", near_groups)
    return (
        new_rows.reshape(NSUPER, nb_rows, width),
        state.reshape(NSUPER, nb_rows, NSUPER * nb),
    )


def solution(mesh):
    in_specs = (
        P("row", "col"),
        P(None, "row", "col"),
        P(None, "row", "col"),
        P(None, "row", None),
        P(),
    )
    out_specs = (P(None, "row", "col"), P(None, "row", None))

    return jax.shard_map(
        per_device, mesh=mesh, in_specs=in_specs, out_specs=out_specs, check_vma=False
    )
```

```python
import jax
import jax.numpy as jnp
from jax import lax
from jax.sharding import PartitionSpec as P


TILE = 128
NSUPER = 3
NEAR = 4


def contract(left, right, left_dim, right_dim, precision=lax.Precision.HIGH):
    return lax.dot_general(
        left,
        right,
        (((left_dim,), (right_dim,)), ((), ())),
        precision=precision,
        preferred_element_type=jnp.float32,
    )


def exchange(blocks, axis, groups=None):
    return lax.all_to_all(blocks, axis, 0, 0, tiled=True, axis_index_groups=groups)


def spread(block, axis, groups=None):
    count = len(groups[0]) if groups else lax.axis_size(axis)
    return exchange(jnp.broadcast_to(block[None], (count,) + block.shape), axis, groups)


def per_device(inverse_sep, sep_panels, chain_panels, diag_inverse, tile_list):
    rows = lax.axis_size("row")
    cols = lax.axis_size("col")
    row = lax.axis_index("row")
    col = lax.axis_index("col")
    height, width = inverse_sep.shape
    nb_cols = sep_panels.shape[2]
    nb_rows = chain_panels.shape[1]
    nb = nb_cols * cols
    cores = cols // rows
    chips = cols // cores
    far = chips // NEAR
    core = col % cores
    chip = col // cores
    tiles = height // TILE
    npair = chain_panels.shape[0]
    slab = NSUPER * nb_cols
    own_rows = NSUPER * nb_rows
    far_groups = [
        [cores * (first + NEAR * i) + c for i in range(far)]
        for first in range(NEAR)
        for c in range(cores)
    ]
    near_groups = [
        [cores * (NEAR * i + j) + c for j in range(NEAR) for c in range(cores)] for i in range(far)
    ]
    swap = [(c, c ^ 1) for c in range(cols)]
    turn = [
        (r * cols + c, (c // cores) * cols + cores * r + c % cores)
        for r in range(rows)
        for c in range(cols)
    ]

    listed = lax.dynamic_slice_in_dim(tile_list, row * tiles, tiles, 1).astype(jnp.float32)
    mask = jnp.broadcast_to(listed[:, :, None], (NSUPER, tiles, TILE)).reshape(NSUPER, 1, height)
    local_panel = (jnp.swapaxes(sep_panels, 1, 2) * mask).reshape(slab, height)
    diag_cols = lax.dynamic_slice_in_dim(diag_inverse, col * nb_cols, nb_cols, 2)
    small = jnp.concatenate([chain_panels, diag_cols], axis=0)
    small_rows = (npair + NSUPER) * nb_cols
    small = jnp.swapaxes(small, 1, 2).reshape(1, small_rows * nb_rows)
    small = spread(small, "row").reshape(rows, small_rows, nb_rows)
    small = jnp.transpose(small, (1, 0, 2)).reshape(small_rows, nb)
    small = lax.optimization_barrier(small)
    chain_cols, diag_cols = small[: npair * nb_cols], small[npair * nb_cols :]
    turned = lax.ppermute(local_panel, ("row", "col"), turn)

    own = lax.all_gather(
        jnp.concatenate([local_panel, chain_cols], axis=1),
        "col",
        axis=0,
        tiled=True,
        axis_index_groups=far_groups,
    )

    left, right = turned[:, :width], turned[:, width:]
    kept = jnp.where(core == 0, left, right)
    other = lax.ppermute(jnp.where(core == 0, right, left), "col", swap)
    pieces = [jnp.where(core == 0, kept, other), jnp.where(core == 0, other, kept)]
    col_panel = spread(jnp.concatenate(pieces, axis=0), "row")
    col_panel = col_panel.reshape(rows, cores, NSUPER, nb_cols, width)

    def from_chip(block, steps):
        moves = [((c + cores * steps[c % cores]) % cols, c) for c in range(cols)]
        return lax.ppermute(block, "col", moves)

    lines = jnp.zeros((far, NSUPER, NEAR, cores, nb_cols, height + nb), jnp.float32)

    def place(lines, block, step, from_core):
        block = block.reshape(far, NSUPER, 1, 1, nb_cols, height + nb)
        start = (0, 0, (chip + step) % NEAR, from_core, 0, 0)
        return lax.dynamic_update_slice(lines, block, start)

    near = [from_chip(own, steps) for steps in ((1, 1), (-1, -1), (2, -2))]
    theirs = lax.ppermute(own, "col", swap)
    lines = place(lines, own, 0, core)
    lines = place(lines, theirs, 0, 1 - core)
    for block, step in zip(near, (1, -1, 2)):
        theirs = lax.ppermute(block, "col", swap)
        lines = place(lines, block, step, core)
        lines = place(lines, theirs, step, 1 - core)
    panel = [lines[:, k, ..., :height].reshape(nb, height) for k in range(NSUPER)]
    chain = [lines[:, p, ..., height:].reshape(nb, nb) for p in range(npair)]

    part = []
    for k in range(NSUPER):
        acc = contract(panel[k], inverse_sep, 1, 0)
        for j in range(k):
            acc = acc + contract(chain[k * (k - 1) // 2 + j], part[j], 1, 0)
        part.append(-acc)
    outgoing = jnp.stack([x.reshape(rows, nb_rows, width) for x in part], axis=1)
    incoming = exchange(outgoing.reshape(rows, own_rows, width), "row")
    new_rows = jnp.sum(incoming, axis=0)

    exact = lax.Precision.HIGHEST
    col_panel = [col_panel[:, :, k].reshape(nb, width) for k in range(NSUPER)]
    solved = []
    for k in range(NSUPER):
        acc = col_panel[k]
        for j in range(k):
            acc = acc - contract(chain[k * (k - 1) // 2 + j], solved[j], 1, 0)
        solved.append(acc)
    solved = jnp.concatenate(solved, axis=0)
    spot = row * nb_rows + lax.broadcasted_iota(jnp.int32, (nb_rows, nb), 0)
    unit = (lax.broadcasted_iota(jnp.int32, (nb_rows, nb), 1) == spot).astype(jnp.float32)
    zero = jnp.zeros((nb_rows, nb), jnp.float32)
    cc = [lax.dynamic_slice_in_dim(chain[p], row * nb_rows, nb_rows, 0) for p in range(npair)]
    lead = [
        jnp.concatenate([unit, -cc[0], contract(cc[2], chain[0], 1, 0, exact) - cc[1]], axis=0),
        jnp.concatenate([zero, unit, -cc[2]], axis=0),
        jnp.concatenate([zero, zero, unit], axis=0),
    ]
    base = []
    for k in range(NSUPER):
        part_lead = lax.dynamic_slice_in_dim(lead[k], col * nb_cols, nb_cols, 1)
        diag_part = diag_cols[k * nb_cols : (k + 1) * nb_cols]
        acc = contract(part_lead, diag_part, 1, 0, exact)
        for j in range(k):
            acc = acc - contract(base[j], chain[k * (k - 1) // 2 + j], 1, 1, exact)
        base.append(acc)
    base = jnp.concatenate(base, axis=1)

    inner = base - contract(new_rows, solved, 1, 1)
    share = own_rows * NSUPER * nb // (NEAR * cores)
    near_sum = jnp.sum(exchange(inner.reshape(NEAR * cores, 1, share), "col", near_groups), axis=0)
    far_sum = jnp.sum(spread(near_sum, "col", far_groups), axis=0)
    state = spread(far_sum, "col", near_groups)
    return (
        new_rows.reshape(NSUPER, nb_rows, width),
        state.reshape(NSUPER, nb_rows, NSUPER * nb),
    )


def solution(mesh):
    in_specs = (
        P("row", "col"),
        P(None, "row", "col"),
        P(None, "row", "col"),
        P(None, "row", None),
        P(),
    )
    out_specs = (P(None, "row", "col"), P(None, "row", None))

    return jax.shard_map(
        per_device, mesh=mesh, in_specs=in_specs, out_specs=out_specs, check_vma=False
    )
```

```python
import jax
import jax.numpy as jnp
from jax import lax
from jax.sharding import PartitionSpec as P


TILE = 128
NSUPER = 3
NEAR = 4


def contract(left, right, left_dim, right_dim, precision=lax.Precision.HIGH):
    return lax.dot_general(
        left,
        right,
        (((left_dim,), (right_dim,)), ((), ())),
        precision=precision,
        preferred_element_type=jnp.float32,
    )


def exchange(blocks, axis, groups=None):
    return lax.all_to_all(blocks, axis, 0, 0, tiled=True, axis_index_groups=groups)


def spread(block, axis, groups=None):
    count = len(groups[0]) if groups else lax.axis_size(axis)
    return exchange(jnp.broadcast_to(block[None], (count,) + block.shape), axis, groups)


def per_device(inverse_sep, sep_panels, chain_panels, diag_inverse, tile_list):
    rows = lax.axis_size("row")
    cols = lax.axis_size("col")
    row = lax.axis_index("row")
    col = lax.axis_index("col")
    height, width = inverse_sep.shape
    nb_cols = sep_panels.shape[2]
    nb_rows = chain_panels.shape[1]
    nb = nb_cols * cols
    cores = cols // rows
    chips = cols // cores
    far = chips // NEAR
    core = col % cores
    chip = col // cores
    tiles = height // TILE
    npair = chain_panels.shape[0]
    slab = NSUPER * nb_cols
    own_rows = NSUPER * nb_rows
    far_groups = [
        [cores * (first + NEAR * i) + c for i in range(far)]
        for first in range(NEAR)
        for c in range(cores)
    ]
    near_groups = [
        [cores * (NEAR * i + j) + c for j in range(NEAR) for c in range(cores)] for i in range(far)
    ]
    swap = [(c, c ^ 1) for c in range(cols)]
    turn = [
        (r * cols + c, (c // cores) * cols + cores * r + c % cores)
        for r in range(rows)
        for c in range(cols)
    ]

    listed = lax.dynamic_slice_in_dim(tile_list, row * tiles, tiles, 1).astype(jnp.float32)
    mask = jnp.broadcast_to(listed[:, :, None], (NSUPER, tiles, TILE)).reshape(NSUPER, 1, height)
    local_panel = (jnp.swapaxes(sep_panels, 1, 2) * mask).reshape(slab, height)
    diag_cols = lax.dynamic_slice_in_dim(diag_inverse, col * nb_cols, nb_cols, 2)
    small = jnp.concatenate([chain_panels, diag_cols], axis=0)
    small_rows = (npair + NSUPER) * nb_cols
    small = jnp.swapaxes(small, 1, 2).reshape(1, small_rows * nb_rows)
    small = spread(small, "row").reshape(rows, small_rows, nb_rows)
    small = jnp.transpose(small, (1, 0, 2)).reshape(small_rows, nb)
    small = lax.optimization_barrier(small)
    chain_cols, diag_cols = small[: npair * nb_cols], small[npair * nb_cols :]
    turned = lax.ppermute(local_panel, ("row", "col"), turn)

    own = lax.all_gather(
        jnp.concatenate([local_panel, chain_cols], axis=1),
        "col",
        axis=0,
        tiled=True,
        axis_index_groups=far_groups,
    )

    left, right = turned[:, :width], turned[:, width:]
    kept = jnp.where(core == 0, left, right)
    other = lax.ppermute(jnp.where(core == 0, right, left), "col", swap)
    pieces = [jnp.where(core == 0, kept, other), jnp.where(core == 0, other, kept)]
    col_panel = spread(jnp.concatenate(pieces, axis=0), "row")
    col_panel = col_panel.reshape(rows, cores, NSUPER, nb_cols, width)

    def from_chip(block, steps):
        moves = [((c + cores * steps[c % cores]) % cols, c) for c in range(cols)]
        return lax.ppermute(block, "col", moves)

    near = [own] + [from_chip(own, steps) for steps in ((1, 1), (2, -2), (-1, -1))]
    mine = jnp.stack(near)
    theirs = lax.ppermute(mine, "col", swap)
    both = jnp.stack([jnp.where(core == 0, mine, theirs), jnp.where(core == 0, theirs, mine)])
    both = both.reshape(cores, NEAR, far, NSUPER, nb_cols, height + nb)
    turnover = chip % NEAR
    places = []
    for place in range(NEAR):
        choice = both[:, place]
        for t in range(1, NEAR):
            choice = jnp.where(turnover == t, both[:, (place - t) % NEAR], choice)
        places.append(choice)
    ordered = jnp.stack(places)
    ordered = jnp.transpose(ordered, (3, 2, 0, 1, 4, 5)).reshape(NSUPER, nb, height + nb)
    panel = [ordered[k, :, :height] for k in range(NSUPER)]
    chain = [ordered[p, :, height:] for p in range(npair)]

    part = []
    for k in range(NSUPER):
        acc = contract(panel[k], inverse_sep, 1, 0)
        for j in range(k):
            acc = acc + contract(chain[k * (k - 1) // 2 + j], part[j], 1, 0)
        part.append(-acc)
    outgoing = jnp.stack([x.reshape(rows, nb_rows, width) for x in part], axis=1)
    incoming = exchange(outgoing.reshape(rows, own_rows, width), "row")
    new_rows = jnp.sum(incoming, axis=0)

    exact = lax.Precision.HIGHEST
    col_panel = [col_panel[:, :, k].reshape(nb, width) for k in range(NSUPER)]
    solved = []
    for k in range(NSUPER):
        acc = col_panel[k]
        for j in range(k):
            acc = acc - contract(chain[k * (k - 1) // 2 + j], solved[j], 1, 0)
        solved.append(acc)
    solved = jnp.concatenate(solved, axis=0)
    spot = row * nb_rows + lax.broadcasted_iota(jnp.int32, (nb_rows, nb), 0)
    unit = (lax.broadcasted_iota(jnp.int32, (nb_rows, nb), 1) == spot).astype(jnp.float32)
    zero = jnp.zeros((nb_rows, nb), jnp.float32)
    cc = [lax.dynamic_slice_in_dim(chain[p], row * nb_rows, nb_rows, 0) for p in range(npair)]
    lead = [
        jnp.concatenate([unit, -cc[0], contract(cc[2], chain[0], 1, 0, exact) - cc[1]], axis=0),
        jnp.concatenate([zero, unit, -cc[2]], axis=0),
        jnp.concatenate([zero, zero, unit], axis=0),
    ]
    base = []
    for k in range(NSUPER):
        part_lead = lax.dynamic_slice_in_dim(lead[k], col * nb_cols, nb_cols, 1)
        diag_part = diag_cols[k * nb_cols : (k + 1) * nb_cols]
        acc = contract(part_lead, diag_part, 1, 0, exact)
        for j in range(k):
            acc = acc - contract(base[j], chain[k * (k - 1) // 2 + j], 1, 1, exact)
        base.append(acc)
    base = jnp.concatenate(base, axis=1)

    inner = base - contract(new_rows, solved, 1, 1)
    share = own_rows * NSUPER * nb // (NEAR * cores)
    near_sum = jnp.sum(exchange(inner.reshape(NEAR * cores, 1, share), "col", near_groups), axis=0)
    far_sum = jnp.sum(spread(near_sum, "col", far_groups), axis=0)
    state = spread(far_sum, "col", near_groups)
    return (
        new_rows.reshape(NSUPER, nb_rows, width),
        state.reshape(NSUPER, nb_rows, NSUPER * nb),
    )


def solution(mesh):
    in_specs = (
        P("row", "col"),
        P(None, "row", "col"),
        P(None, "row", "col"),
        P(None, "row", None),
        P(),
    )
    out_specs = (P(None, "row", "col"), P(None, "row", None))

    return jax.shard_map(
        per_device, mesh=mesh, in_specs=in_specs, out_specs=out_specs, check_vma=False
    )
```

```python
import jax
import jax.numpy as jnp
from jax import lax
from jax.sharding import PartitionSpec as P


TILE = 128
NSUPER = 3
NEAR = 4


def contract(left, right, left_dim, right_dim, precision=lax.Precision.HIGH):
    return lax.dot_general(
        left,
        right,
        (((left_dim,), (right_dim,)), ((), ())),
        precision=precision,
        preferred_element_type=jnp.float32,
    )


def exchange(blocks, axis, groups=None):
    return lax.all_to_all(blocks, axis, 0, 0, tiled=True, axis_index_groups=groups)


def spread(block, axis, groups=None):
    count = len(groups[0]) if groups else lax.axis_size(axis)
    return exchange(jnp.broadcast_to(block[None], (count,) + block.shape), axis, groups)


def per_device(inverse_sep, sep_panels, chain_panels, diag_inverse, tile_list):
    rows = lax.axis_size("row")
    cols = lax.axis_size("col")
    row = lax.axis_index("row")
    col = lax.axis_index("col")
    height, width = inverse_sep.shape
    nb_cols = sep_panels.shape[2]
    nb_rows = chain_panels.shape[1]
    nb = nb_cols * cols
    cores = cols // rows
    chips = cols // cores
    far = chips // NEAR
    core = col % cores
    chip = col // cores
    tiles = height // TILE
    npair = chain_panels.shape[0]
    slab = NSUPER * nb_cols
    own_rows = NSUPER * nb_rows
    far_groups = [
        [cores * (first + NEAR * i) + c for i in range(far)]
        for first in range(NEAR)
        for c in range(cores)
    ]
    far_chips = [
        [cores * (first + NEAR * i) + c for i in range(far) for c in range(cores)]
        for first in range(NEAR)
    ]
    near_groups = [
        [cores * (NEAR * i + j) + c for j in range(NEAR) for c in range(cores)] for i in range(far)
    ]
    swap = [(c, c ^ 1) for c in range(cols)]
    turn = [
        (r * cols + c, (c // cores) * cols + cores * r + c % cores)
        for r in range(rows)
        for c in range(cols)
    ]

    listed = lax.dynamic_slice_in_dim(tile_list, row * tiles, tiles, 1).astype(jnp.float32)
    mask = jnp.broadcast_to(listed[:, :, None], (NSUPER, tiles, TILE)).reshape(NSUPER, 1, height)
    local_panel = (jnp.swapaxes(sep_panels, 1, 2) * mask).reshape(slab, height)
    diag_cols = lax.dynamic_slice_in_dim(diag_inverse, col * nb_cols, nb_cols, 2)
    small = jnp.concatenate([chain_panels, diag_cols], axis=0)
    small_rows = (npair + NSUPER) * nb_cols
    small = jnp.swapaxes(small, 1, 2).reshape(1, small_rows * nb_rows)
    small = spread(small, "row").reshape(rows, small_rows, nb_rows)
    small = jnp.transpose(small, (1, 0, 2)).reshape(small_rows, nb)
    small = lax.optimization_barrier(small)
    chain_cols, diag_cols = small[: npair * nb_cols], small[npair * nb_cols :]
    turned = lax.ppermute(local_panel, ("row", "col"), turn)

    own = lax.all_gather(
        jnp.concatenate([local_panel, chain_cols], axis=1),
        "col",
        axis=0,
        tiled=True,
        axis_index_groups=far_chips,
    )

    left, right = turned[:, :width], turned[:, width:]
    kept = jnp.where(core == 0, left, right)
    other = lax.ppermute(jnp.where(core == 0, right, left), "col", swap)
    pieces = [jnp.where(core == 0, kept, other), jnp.where(core == 0, other, kept)]
    col_panel = spread(jnp.concatenate(pieces, axis=0), "row")
    col_panel = col_panel.reshape(rows, cores, NSUPER, nb_cols, width)

    def from_chip(block, steps):
        moves = [((c + cores * steps[c % cores]) % cols, c) for c in range(cols)]
        return lax.ppermute(block, "col", moves)

    wide = height + nb
    own = own.reshape(far, cores, slab, wide)
    half = jnp.where(core == 0, own[:, 0], own[:, 1]).reshape(far * slab, wide)
    beside = from_chip(own.reshape(far * cores * slab, wide), (1, -1))
    across = from_chip(half, (2, -2))
    beside_other = lax.ppermute(beside, "col", swap)
    across_other = lax.ppermute(across, "col", swap)
    shape = (far, cores, NSUPER, nb_cols, wide)
    after = jnp.where(core == 0, beside, beside_other).reshape(shape)
    before = jnp.where(core == 0, beside_other, beside).reshape(shape)
    halves = [
        jnp.where(core == 0, across, across_other).reshape(far, slab, wide),
        jnp.where(core == 0, across_other, across).reshape(far, slab, wide),
    ]
    blocks = [own.reshape(shape), after, jnp.stack(halves, axis=1).reshape(shape), before]
    turnover = chip % NEAR
    places = []
    for place in range(NEAR):
        choice = blocks[place]
        for t in range(1, NEAR):
            choice = jnp.where(turnover == t, blocks[(place - t) % NEAR], choice)
        places.append(choice)
    ordered = jnp.stack(places)
    ordered = jnp.transpose(ordered, (3, 1, 0, 2, 4, 5)).reshape(NSUPER, nb, wide)
    panel = [ordered[k, :, :height] for k in range(NSUPER)]
    chain = [ordered[p, :, height:] for p in range(npair)]

    part = []
    for k in range(NSUPER):
        acc = contract(panel[k], inverse_sep, 1, 0)
        for j in range(k):
            acc = acc + contract(chain[k * (k - 1) // 2 + j], part[j], 1, 0)
        part.append(-acc)
    outgoing = jnp.stack([x.reshape(rows, nb_rows, width) for x in part], axis=1)
    incoming = exchange(outgoing.reshape(rows, own_rows, width), "row")
    new_rows = jnp.sum(incoming, axis=0)

    exact = lax.Precision.HIGHEST
    col_panel = [col_panel[:, :, k].reshape(nb, width) for k in range(NSUPER)]
    solved = []
    for k in range(NSUPER):
        acc = col_panel[k]
        for j in range(k):
            acc = acc - contract(chain[k * (k - 1) // 2 + j], solved[j], 1, 0)
        solved.append(acc)
    solved = jnp.concatenate(solved, axis=0)
    spot = row * nb_rows + lax.broadcasted_iota(jnp.int32, (nb_rows, nb), 0)
    unit = (lax.broadcasted_iota(jnp.int32, (nb_rows, nb), 1) == spot).astype(jnp.float32)
    zero = jnp.zeros((nb_rows, nb), jnp.float32)
    cc = [lax.dynamic_slice_in_dim(chain[p], row * nb_rows, nb_rows, 0) for p in range(npair)]
    lead = [
        jnp.concatenate([unit, -cc[0], contract(cc[2], chain[0], 1, 0, exact) - cc[1]], axis=0),
        jnp.concatenate([zero, unit, -cc[2]], axis=0),
        jnp.concatenate([zero, zero, unit], axis=0),
    ]
    base = []
    for k in range(NSUPER):
        part_lead = lax.dynamic_slice_in_dim(lead[k], col * nb_cols, nb_cols, 1)
        diag_part = diag_cols[k * nb_cols : (k + 1) * nb_cols]
        acc = contract(part_lead, diag_part, 1, 0, exact)
        for j in range(k):
            acc = acc - contract(base[j], chain[k * (k - 1) // 2 + j], 1, 1, exact)
        base.append(acc)
    base = jnp.concatenate(base, axis=1)

    inner = base - contract(new_rows, solved, 1, 1)
    share = own_rows * NSUPER * nb // (NEAR * cores)
    near_sum = jnp.sum(exchange(inner.reshape(NEAR * cores, 1, share), "col", near_groups), axis=0)
    far_sum = jnp.sum(spread(near_sum, "col", far_groups), axis=0)
    state = spread(far_sum, "col", near_groups)
    return (
        new_rows.reshape(NSUPER, nb_rows, width),
        state.reshape(NSUPER, nb_rows, NSUPER * nb),
    )


def solution(mesh):
    in_specs = (
        P("row", "col"),
        P(None, "row", "col"),
        P(None, "row", "col"),
        P(None, "row", None),
        P(),
    )
    out_specs = (P(None, "row", "col"), P(None, "row", None))

    return jax.shard_map(
        per_device, mesh=mesh, in_specs=in_specs, out_specs=out_specs, check_vma=False
    )
```

```python
import jax
import jax.numpy as jnp
from jax import lax
from jax.sharding import PartitionSpec as P


TILE = 128
NSUPER = 3
NEAR = 4


def contract(left, right, left_dim, right_dim, precision=lax.Precision.HIGH):
    return lax.dot_general(
        left,
        right,
        (((left_dim,), (right_dim,)), ((), ())),
        precision=precision,
        preferred_element_type=jnp.float32,
    )


def exchange(blocks, axis, groups=None):
    return lax.all_to_all(blocks, axis, 0, 0, tiled=True, axis_index_groups=groups)


def spread(block, axis, groups=None):
    count = len(groups[0]) if groups else lax.axis_size(axis)
    return exchange(jnp.broadcast_to(block[None], (count,) + block.shape), axis, groups)


def per_device(inverse_sep, sep_panels, chain_panels, diag_inverse, tile_list):
    rows = lax.axis_size("row")
    cols = lax.axis_size("col")
    row = lax.axis_index("row")
    col = lax.axis_index("col")
    height, width = inverse_sep.shape
    nb_cols = sep_panels.shape[2]
    nb_rows = chain_panels.shape[1]
    nb = nb_cols * cols
    cores = cols // rows
    chips = cols // cores
    far = chips // NEAR
    core = col % cores
    chip = col // cores
    tiles = height // TILE
    npair = chain_panels.shape[0]
    slab = NSUPER * nb_cols
    own_rows = NSUPER * nb_rows
    far_groups = [
        [cores * (first + NEAR * i) + c for i in range(far)]
        for first in range(NEAR)
        for c in range(cores)
    ]
    far_chips = [
        [cores * (first + NEAR * i) + c for i in range(far) for c in range(cores)]
        for first in range(NEAR)
    ]
    near_groups = [
        [cores * (NEAR * i + j) + c for j in range(NEAR) for c in range(cores)] for i in range(far)
    ]
    swap = [(c, c ^ 1) for c in range(cols)]
    turn = [
        (r * cols + c, (c // cores) * cols + cores * r + c % cores)
        for r in range(rows)
        for c in range(cols)
    ]

    listed = lax.dynamic_slice_in_dim(tile_list, row * tiles, tiles, 1).astype(jnp.float32)
    mask = jnp.broadcast_to(listed[:, :, None], (NSUPER, tiles, TILE)).reshape(NSUPER, 1, height)
    local_panel = (jnp.swapaxes(sep_panels, 1, 2) * mask).reshape(slab, height)
    diag_cols = lax.dynamic_slice_in_dim(diag_inverse, col * nb_cols, nb_cols, 2)
    small = jnp.concatenate([chain_panels, diag_cols], axis=0)
    small_rows = (npair + NSUPER) * nb_cols
    small = jnp.swapaxes(small, 1, 2).reshape(1, small_rows * nb_rows)
    small = spread(small, "row").reshape(rows, small_rows, nb_rows)
    small = jnp.transpose(small, (1, 0, 2)).reshape(small_rows, nb)
    small = lax.optimization_barrier(small)
    chain_cols, diag_cols = small[: npair * nb_cols], small[npair * nb_cols :]
    turned = lax.ppermute(local_panel, ("row", "col"), turn)

    own = lax.all_gather(
        jnp.concatenate([local_panel, chain_cols], axis=1),
        "col",
        axis=0,
        tiled=True,
        axis_index_groups=far_chips,
    )

    plane_groups = [
        [r * cols + cores * z + c for r in range(rows) for c in range(cores)] for z in range(chips)
    ]
    pieces = jnp.stack([turned[:, c * width : (c + 1) * width] for c in range(cores)])
    pieces = jnp.broadcast_to(pieces[None], (rows, cores, slab, width))
    pieces = pieces.reshape(rows * cores, slab, width)
    col_panel = exchange(pieces, ("row", "col"), plane_groups)
    col_panel = col_panel.reshape(rows, cores, NSUPER, nb_cols, width)

    def from_chip(block, steps):
        moves = [((c + cores * steps[c % cores]) % cols, c) for c in range(cols)]
        return lax.ppermute(block, "col", moves)

    wide = height + nb
    own = own.reshape(far, cores, slab, wide)
    half = jnp.where(core == 0, own[:, 0], own[:, 1]).reshape(far * slab, wide)
    beside = from_chip(own.reshape(far * cores * slab, wide), (1, -1))
    across = from_chip(half, (2, -2))
    beside_other = lax.ppermute(beside, "col", swap)
    across_other = lax.ppermute(across, "col", swap)
    shape = (far, cores, NSUPER, nb_cols, wide)
    after = jnp.where(core == 0, beside, beside_other).reshape(shape)
    before = jnp.where(core == 0, beside_other, beside).reshape(shape)
    halves = [
        jnp.where(core == 0, across, across_other).reshape(far, slab, wide),
        jnp.where(core == 0, across_other, across).reshape(far, slab, wide),
    ]
    blocks = [own.reshape(shape), after, jnp.stack(halves, axis=1).reshape(shape), before]
    turnover = chip % NEAR
    places = []
    for place in range(NEAR):
        choice = blocks[place]
        for t in range(1, NEAR):
            choice = jnp.where(turnover == t, blocks[(place - t) % NEAR], choice)
        places.append(choice)
    ordered = jnp.stack(places)
    ordered = jnp.transpose(ordered, (3, 1, 0, 2, 4, 5)).reshape(NSUPER, nb, wide)
    panel = [ordered[k, :, :height] for k in range(NSUPER)]
    chain = [ordered[p, :, height:] for p in range(npair)]

    part = []
    for k in range(NSUPER):
        acc = contract(panel[k], inverse_sep, 1, 0)
        for j in range(k):
            acc = acc + contract(chain[k * (k - 1) // 2 + j], part[j], 1, 0)
        part.append(-acc)
    outgoing = jnp.stack([x.reshape(rows, nb_rows, width) for x in part], axis=1)
    incoming = exchange(outgoing.reshape(rows, own_rows, width), "row")
    new_rows = jnp.sum(incoming, axis=0)

    exact = lax.Precision.HIGHEST
    col_panel = [col_panel[:, :, k].reshape(nb, width) for k in range(NSUPER)]
    solved = []
    for k in range(NSUPER):
        acc = col_panel[k]
        for j in range(k):
            acc = acc - contract(chain[k * (k - 1) // 2 + j], solved[j], 1, 0)
        solved.append(acc)
    solved = jnp.concatenate(solved, axis=0)
    spot = row * nb_rows + lax.broadcasted_iota(jnp.int32, (nb_rows, nb), 0)
    unit = (lax.broadcasted_iota(jnp.int32, (nb_rows, nb), 1) == spot).astype(jnp.float32)
    zero = jnp.zeros((nb_rows, nb), jnp.float32)
    cc = [lax.dynamic_slice_in_dim(chain[p], row * nb_rows, nb_rows, 0) for p in range(npair)]
    lead = [
        jnp.concatenate([unit, -cc[0], contract(cc[2], chain[0], 1, 0, exact) - cc[1]], axis=0),
        jnp.concatenate([zero, unit, -cc[2]], axis=0),
        jnp.concatenate([zero, zero, unit], axis=0),
    ]
    base = []
    for k in range(NSUPER):
        part_lead = lax.dynamic_slice_in_dim(lead[k], col * nb_cols, nb_cols, 1)
        diag_part = diag_cols[k * nb_cols : (k + 1) * nb_cols]
        acc = contract(part_lead, diag_part, 1, 0, exact)
        for j in range(k):
            acc = acc - contract(base[j], chain[k * (k - 1) // 2 + j], 1, 1, exact)
        base.append(acc)
    base = jnp.concatenate(base, axis=1)

    inner = base - contract(new_rows, solved, 1, 1)
    share = own_rows * NSUPER * nb // (NEAR * cores)
    near_sum = jnp.sum(exchange(inner.reshape(NEAR * cores, 1, share), "col", near_groups), axis=0)
    far_sum = jnp.sum(spread(near_sum, "col", far_groups), axis=0)
    state = spread(far_sum, "col", near_groups)
    return (
        new_rows.reshape(NSUPER, nb_rows, width),
        state.reshape(NSUPER, nb_rows, NSUPER * nb),
    )


def solution(mesh):
    in_specs = (
        P("row", "col"),
        P(None, "row", "col"),
        P(None, "row", "col"),
        P(None, "row", None),
        P(),
    )
    out_specs = (P(None, "row", "col"), P(None, "row", None))

    return jax.shard_map(
        per_device, mesh=mesh, in_specs=in_specs, out_specs=out_specs, check_vma=False
    )
```

```python
import jax
import jax.numpy as jnp
from jax import lax
from jax.sharding import PartitionSpec as P


TILE = 128
NSUPER = 3
NEAR = 4


def contract(left, right, left_dim, right_dim, precision=lax.Precision.HIGH):
    return lax.dot_general(
        left,
        right,
        (((left_dim,), (right_dim,)), ((), ())),
        precision=precision,
        preferred_element_type=jnp.float32,
    )


def exchange(blocks, axis, groups=None):
    return lax.all_to_all(blocks, axis, 0, 0, tiled=True, axis_index_groups=groups)


def spread(block, axis, groups=None):
    count = len(groups[0]) if groups else lax.axis_size(axis)
    return exchange(jnp.broadcast_to(block[None], (count,) + block.shape), axis, groups)


def per_device(inverse_sep, sep_panels, chain_panels, diag_inverse, tile_list):
    rows = lax.axis_size("row")
    cols = lax.axis_size("col")
    row = lax.axis_index("row")
    col = lax.axis_index("col")
    height, width = inverse_sep.shape
    nb_cols = sep_panels.shape[2]
    nb_rows = chain_panels.shape[1]
    nb = nb_cols * cols
    cores = cols // rows
    chips = cols // cores
    far = chips // NEAR
    core = col % cores
    chip = col // cores
    tiles = height // TILE
    npair = chain_panels.shape[0]
    slab = NSUPER * nb_cols
    own_rows = NSUPER * nb_rows
    far_groups = [
        [cores * (first + NEAR * i) + c for i in range(far)]
        for first in range(NEAR)
        for c in range(cores)
    ]
    far_chips = [
        [cores * (first + NEAR * i) + c for i in range(far) for c in range(cores)]
        for first in range(NEAR)
    ]
    near_groups = [
        [cores * (NEAR * i + j) + c for j in range(NEAR) for c in range(cores)] for i in range(far)
    ]
    swap = [(c, c ^ 1) for c in range(cols)]
    turn = [
        (r * cols + c, (c // cores) * cols + cores * r + c % cores)
        for r in range(rows)
        for c in range(cols)
    ]

    listed = lax.dynamic_slice_in_dim(tile_list, row * tiles, tiles, 1).astype(jnp.float32)
    mask = jnp.broadcast_to(listed[:, :, None], (NSUPER, tiles, TILE)).reshape(NSUPER, 1, height)
    local_panel = (jnp.swapaxes(sep_panels, 1, 2) * mask).reshape(slab, height)
    diag_cols = lax.dynamic_slice_in_dim(diag_inverse, col * nb_cols, nb_cols, 2)
    small = jnp.concatenate([chain_panels, diag_cols], axis=0)
    small_rows = (npair + NSUPER) * nb_cols
    small = jnp.swapaxes(small, 1, 2).reshape(1, small_rows * nb_rows)
    small = spread(small, "row").reshape(rows, small_rows, nb_rows)
    small = jnp.transpose(small, (1, 0, 2)).reshape(small_rows, nb)
    small = lax.optimization_barrier(small)
    chain_cols, diag_cols = small[: npair * nb_cols], small[npair * nb_cols :]
    turned = lax.ppermute(local_panel, ("row", "col"), turn)

    own = lax.all_gather(
        jnp.concatenate([local_panel, chain_cols], axis=1),
        "col",
        axis=0,
        tiled=True,
        axis_index_groups=far_chips,
    )

    plane_groups = [
        [r * cols + cores * z + c for r in range(rows) for c in range(cores)] for z in range(chips)
    ]
    pieces = jnp.stack([turned[:, c * width : (c + 1) * width] for c in range(cores)])
    pieces = jnp.broadcast_to(pieces[None], (rows, cores, slab, width))
    pieces = pieces.reshape(rows * cores, slab, width)
    col_panel = exchange(pieces, ("row", "col"), plane_groups)
    col_panel = col_panel.reshape(rows, cores, NSUPER, nb_cols, width)

    def from_chip(block, steps):
        moves = [((c + cores * steps[c % cores]) % cols, c) for c in range(cols)]
        return lax.ppermute(block, "col", moves)

    wide = height + nb
    own = own.reshape(far, cores, slab, wide)
    half = jnp.where(core == 0, own[:, 0], own[:, 1]).reshape(far * slab, wide)
    beside = from_chip(own.reshape(far * cores * slab, wide), (1, -1))
    across = from_chip(half, (2, -2))
    beside_other = lax.ppermute(beside, "col", swap)
    across_other = lax.ppermute(across, "col", swap)
    shape = (far, cores, NSUPER, nb_cols, wide)
    halves = [
        jnp.where(core == 0, across, across_other).reshape(far, slab, wide),
        jnp.where(core == 0, across_other, across).reshape(far, slab, wide),
    ]
    two = jnp.stack(halves, axis=1).reshape(shape)
    first = core == 0
    places = []
    for place in range(NEAR):
        delta = (place - chip) % NEAR
        from_beside = jnp.where(first, delta == 1, delta == NEAR - 1)
        from_other = jnp.where(first, delta == NEAR - 1, delta == 1)
        choice = jnp.where(from_other, beside_other.reshape(shape), two)
        choice = jnp.where(from_beside, beside.reshape(shape), choice)
        places.append(jnp.where(delta == 0, own.reshape(shape), choice))
    ordered = jnp.stack(places)
    ordered = jnp.transpose(ordered, (3, 1, 0, 2, 4, 5)).reshape(NSUPER, nb, wide)
    panel = [ordered[k, :, :height] for k in range(NSUPER)]
    chain = [ordered[p, :, height:] for p in range(npair)]

    part = []
    for k in range(NSUPER):
        acc = contract(panel[k], inverse_sep, 1, 0)
        for j in range(k):
            acc = acc + contract(chain[k * (k - 1) // 2 + j], part[j], 1, 0)
        part.append(-acc)
    outgoing = jnp.stack([x.reshape(rows, nb_rows, width) for x in part], axis=1)
    incoming = exchange(outgoing.reshape(rows, own_rows, width), "row")
    new_rows = jnp.sum(incoming, axis=0)

    exact = lax.Precision.HIGH
    col_panel = [col_panel[:, :, k].reshape(nb, width) for k in range(NSUPER)]
    solved = []
    for k in range(NSUPER):
        acc = col_panel[k]
        for j in range(k):
            acc = acc - contract(chain[k * (k - 1) // 2 + j], solved[j], 1, 0)
        solved.append(acc)
    solved = jnp.concatenate(solved, axis=0)
    spot = row * nb_rows + lax.broadcasted_iota(jnp.int32, (nb_rows, nb), 0)
    unit = (lax.broadcasted_iota(jnp.int32, (nb_rows, nb), 1) == spot).astype(jnp.float32)
    zero = jnp.zeros((nb_rows, nb), jnp.float32)
    cc = [lax.dynamic_slice_in_dim(chain[p], row * nb_rows, nb_rows, 0) for p in range(npair)]
    lead = [
        jnp.concatenate([unit, -cc[0], contract(cc[2], chain[0], 1, 0, exact) - cc[1]], axis=0),
        jnp.concatenate([zero, unit, -cc[2]], axis=0),
        jnp.concatenate([zero, zero, unit], axis=0),
    ]
    base = []
    for k in range(NSUPER):
        part_lead = lax.dynamic_slice_in_dim(lead[k], col * nb_cols, nb_cols, 1)
        diag_part = diag_cols[k * nb_cols : (k + 1) * nb_cols]
        acc = contract(part_lead, diag_part, 1, 0, exact)
        for j in range(k):
            acc = acc - contract(base[j], chain[k * (k - 1) // 2 + j], 1, 1, exact)
        base.append(acc)
    base = jnp.concatenate(base, axis=1)

    inner = base - contract(new_rows, solved, 1, 1)
    share = own_rows * NSUPER * nb // (NEAR * cores)
    near_sum = jnp.sum(exchange(inner.reshape(NEAR * cores, 1, share), "col", near_groups), axis=0)
    far_sum = jnp.sum(spread(near_sum, "col", far_groups), axis=0)
    state = spread(far_sum, "col", near_groups)
    return (
        new_rows.reshape(NSUPER, nb_rows, width),
        state.reshape(NSUPER, nb_rows, NSUPER * nb),
    )


def solution(mesh):
    in_specs = (
        P("row", "col"),
        P(None, "row", "col"),
        P(None, "row", "col"),
        P(None, "row", None),
        P(),
    )
    out_specs = (P(None, "row", "col"), P(None, "row", None))

    return jax.shard_map(
        per_device, mesh=mesh, in_specs=in_specs, out_specs=out_specs, check_vma=False
    )
```
